32 devices in a mesh: seq: 8 (over z, y), pat: 4 (over x, core).
Axes of the slice: x: 2, y: 2, z: 4, core: 2. Of those that a mesh axis runs over, the one named last changes fastest.
Arguments:
- queries: bfloat16 [4, 2048, 2048], P('pat', 'seq'), may hold values from -6 to 6
- key_rows: bfloat16 [4, 2048, 2048], P('pat', 'seq'), may hold values from -6 to 6
- value_rows: bfloat16 [4, 2048, 2048], P('pat', 'seq'), may hold values from -6 to 6
- out_weight: bfloat16 [2048, 2048], P('pat'), may hold values from -0.125 to 0.125
- grad_out: bfloat16 [4, 2048, 2048], P('pat', 'seq'), may hold values from -6 to 6
- visit_mask: int32 [4, 8, 2, 2], P('pat', 'seq'), may hold values 0 or 1
- lengths: int32 [4], P('pat'), may hold values from 256 to 2048, as said below
Outputs:
- mixed: bfloat16 [4, 2048, 2048], P('pat', 'seq')
- query_grad: bfloat16 [4, 2048, 2048], P('pat', 'seq')
- key_grad: bfloat16 [4, 2048, 2048], P('pat', 'seq')
- value_grad: bfloat16 [4, 2048, 2048], P('pat', 'seq')
- weight_grad: float32 [2048, 2048], P('pat', 'seq')
The draws below stay inside these ranges and needn't reach their ends.
Inputs may be any that keep to these rules, and one draw needn't show every extreme that they name: `lengths`: one patient's record fills all 2048 positions in every draw.
All inputs are finite; a program needn't handle non-finite values. No bound on the sum of `visit_mask` on one device may be relied on, other than what follows from the above.
Results may differ from the reference program's by a relative error of at most 0.013.
Values may be sent and summed in bfloat16 or wider, within the bound.
A program may use at most 384 MiB of HBM per device.

```python
import math
import jax
import jax.numpy as jnp
from jax import lax

H = 16
HD = 128
D = 2048
TOK_DEV = 256
NB = 2
GROUPS = 8
LEN = 2048
PATS = 4
N_SEQ = 8


def draw_lengths(key, part):
    base_key, pick_key = jax.random.split(jax.random.fold_in(key, 7))
    drawn = jax.random.randint(base_key, (PATS,), LEN // 8, LEN + 1)
    chosen = jax.random.randint(pick_key, (), 0, PATS)
    return jnp.where(jnp.arange(PATS) == chosen, LEN, drawn).astype(jnp.int32)


def with_ends(values, rng, low, top_value):
    index_at = [jax.random.randint(jax.random.fold_in(rng, axis), (), 0, length) for axis, length in enumerate(values.shape)]
    widest = values.shape.index(max(values.shape))
    next_to = index_at[:widest] + [(index_at[widest] + 1) % values.shape[widest]] + index_at[widest + 1:]
    return values.at[tuple(index_at)].set(low).at[tuple(next_to)].set(top_value)


def with_spikes(values, stream_key, source, target, shards_of, factor):
    def block_of(axis_at):
        return (jnp.arange(values.shape[axis_at]) // (values.shape[axis_at] // shards_of)).reshape((-1,) + (1,) * (values.ndim - 1 - axis_at))

    one_side = jax.random.permutation(stream_key, shards_of)[block_of(target)]
    far = (block_of(target) + shards_of // 2) % shards_of
    return jnp.where((block_of(source) == one_side) | (block_of(source) == far), factor * values, values)


def steps_of(stream_key, dims, cuts, low, largest):
    level, own = 1.0, jax.random.fold_in(stream_key, 6)
    for position, blocks in cuts:
        draws = jnp.exp(jax.random.uniform(jax.random.fold_in(own, position), (blocks,), jnp.float32, low / len(cuts), largest / len(cuts)))
        level = level * jnp.repeat(draws, dims[position] // blocks).reshape([-1 if axis == position else 1 for axis in range(len(dims))])
    return level


def centred(key, shape, scale, limit, cuts=(), held_as=jnp.bfloat16):
    values = scale * jax.random.normal(key, shape, jnp.float32)
    if cuts:
        values = values * steps_of(key, shape, cuts, -0.22, 0.18)
    return jnp.clip(values, -limit, limit).astype(held_as)


def bell_draw_with(own_key, extent, deviation, limit, shards, heavy, kind=jnp.bfloat16):
    values = deviation * jax.random.normal(own_key, extent, jnp.float32)
    if shards:
        values = values * steps_of(own_key, extent, shards, -0.22, 0.18)
    return jnp.clip(with_spikes(values, jax.random.fold_in(own_key, 3), *heavy), -limit, limit).astype(kind)


def setup_inputs(seed: int = 0) -> dict:
    splits = jax.random.split(jax.random.key(seed), 8)
    queries = centred(splits[0], (PATS, LEN, D), 1.0, 6.0, ((0, 4), (1, 8)))
    key_rows = centred(splits[1], (PATS, LEN, D), 1.0, 6.0, ((0, 4), (1, 8)))
    value_rows = centred(splits[2], (PATS, LEN, D), 1.0, 6.0, ((0, 4), (1, 8)))
    out_weight = centred(splits[3], (D, D), D ** -0.5, 0.125, ((0, 4),))
    grad_out = bell_draw_with(splits[4], (PATS, LEN, D), 1.0, 6.0, ((0, 4), (1, 8)), (1, 2, 8, 2.0))
    visit_mask = with_ends((jax.random.randint(splits[5], (PATS, GROUPS, NB, NB), 0, 2) < 1).astype(jnp.int32), jax.random.fold_in(splits[5], 1), 0, 1)
    lengths = draw_lengths(jax.random.fold_in(splits[7], 71), 0)
    return {"queries": queries, "key_rows": key_rows, "value_rows": value_rows, "out_weight": out_weight, "grad_out": grad_out, "visit_mask": visit_mask, "lengths": lengths}


def pair_mask(block_mask, live_mask, row_count):
    block_count = block_mask.shape[0]
    block_rows = row_count // block_count
    block_grid = jnp.repeat(jnp.repeat(block_mask, block_rows, axis=0), block_rows, axis=1)
    row_index = jnp.arange(row_count, dtype=jnp.int32)
    same_block = row_index[:, None] // block_rows == row_index[None, :] // block_rows
    causal = row_index[:, None] >= row_index[None, :]
    keep_mask = causal & (same_block | (block_grid == 1))
    return keep_mask.astype(jnp.float32) * live_mask[:, None] * live_mask[None, :]

def group_pass(query_rows, key_rows, value_rows, scaled_grad, live_mask, row_scale, allowed, state_before, state_after):
    head_count = state_before.shape[0]
    head_dim = state_before.shape[1]
    row_count = query_rows.shape[0]
    query_heads = query_rows.reshape(row_count, head_count, head_dim)
    key_heads = key_rows.reshape(row_count, head_count, head_dim)
    value_heads = value_rows.reshape(row_count, head_count, head_dim)
    grad_heads = scaled_grad.reshape(row_count, head_count, head_dim)
    highest = lax.Precision.HIGHEST
    scores = jnp.einsum('thd,shd->hts', query_heads, key_heads, preferred_element_type=jnp.float32) * allowed[None]
    score_half = scores.astype(jnp.bfloat16)
    within = jnp.einsum('hts,she->the', score_half, value_heads, preferred_element_type=jnp.float32)
    carried = jnp.einsum('thd,hde->the', query_heads.astype(jnp.float32), state_before, precision=highest)
    attended = (row_scale[:, None, None] * (within + carried)).reshape(row_count, -1).astype(jnp.bfloat16)
    grad_scores = jnp.einsum('the,she->hts', grad_heads, value_heads, preferred_element_type=jnp.float32) * allowed[None]
    grad_half = grad_scores.astype(jnp.bfloat16)
    query_grad = jnp.einsum('hts,shd->thd', grad_half, key_heads, preferred_element_type=jnp.float32)
    query_grad = query_grad + jnp.einsum('the,hde->thd', grad_heads.astype(jnp.float32), state_before, precision=highest)
    key_grad = jnp.einsum('hts,thd->shd', grad_half, query_heads, preferred_element_type=jnp.float32)
    key_grad = key_grad + live_mask[:, None, None] * jnp.einsum('she,hde->shd', value_heads.astype(jnp.float32), state_after, precision=highest)
    value_grad = jnp.einsum('hts,the->she', score_half, grad_heads, preferred_element_type=jnp.float32)
    value_grad = value_grad + live_mask[:, None, None] * jnp.einsum('shd,hde->she', key_heads.astype(jnp.float32), state_after, precision=highest)
    return (attended, query_grad.reshape(row_count, -1).astype(jnp.bfloat16), key_grad.reshape(row_count, -1).astype(jnp.bfloat16), value_grad.reshape(row_count, -1).astype(jnp.bfloat16))

def reference(queries, key_rows, value_rows, out_weight, grad_out, visit_mask, lengths):
    group_total = N_SEQ
    row_count = TOK_DEV
    flat_grad = grad_out.reshape(PATS * LEN, D)
    grad_attended = lax.dot_general(flat_grad, out_weight, (((1,), (1,)), ((), ())), preferred_element_type=jnp.float32).astype(jnp.bfloat16)
    grad_attended = grad_attended.reshape(PATS, group_total, row_count, D)

    def one_patient(inputs):
        query_p, key_p, value_p, grad_p, mask_p, length = inputs
        query_c = query_p.reshape(group_total, row_count, D)
        key_c = key_p.reshape(group_total, row_count, D)
        value_c = value_p.reshape(group_total, row_count, D)
        positions = jnp.arange(LEN, dtype=jnp.int32).reshape(group_total, row_count)
        live_mask = (positions < length).astype(jnp.float32)
        row_scale = live_mask * lax.rsqrt((positions + 1).astype(jnp.float32)) / math.sqrt(HD)
        scaled_grad = (row_scale[:, :, None] * grad_p.astype(jnp.float32)).astype(jnp.bfloat16)
        kept_keys = (key_c * live_mask[:, :, None].astype(jnp.bfloat16)).reshape(group_total, row_count, H, HD)
        state_local = jnp.einsum('cshd,cshe->chde', kept_keys, value_c.reshape(group_total, row_count, H, HD), preferred_element_type=jnp.float32)
        reverse_local = jnp.einsum('cthd,cthe->chde', query_c.reshape(group_total, row_count, H, HD), scaled_grad.reshape(group_total, row_count, H, HD), preferred_element_type=jnp.float32)
        zero_state = jnp.zeros((1, H, HD, HD), jnp.float32)
        state_before = jnp.concatenate([zero_state, jnp.cumsum(state_local, axis=0)[:-1]], axis=0)
        suffix_sums = jnp.cumsum(reverse_local[::-1], axis=0)[::-1]
        state_after = jnp.concatenate([suffix_sums[1:], zero_state], axis=0)

        def one_group(pieces):
            q_rows, k_rows, v_rows, g_rows, block_mask, live_c, scale_c, before_c, after_c = pieces
            allowed = pair_mask(block_mask, live_c, row_count)
            return group_pass(q_rows, k_rows, v_rows, g_rows, live_c, scale_c, allowed, before_c, after_c)
        return lax.map(one_group, (query_c, key_c, value_c, scaled_grad, mask_p, live_mask, row_scale, state_before, state_after))
    attended, query_grad, key_grad, value_grad = lax.map(one_patient, (queries, key_rows, value_rows, grad_attended, visit_mask, lengths))
    flat_attended = attended.reshape(PATS * LEN, D)
    mixed = jnp.dot(flat_attended, out_weight, preferred_element_type=jnp.float32).astype(jnp.bfloat16)
    weight_grad = lax.dot_general(flat_attended, flat_grad, (((0,), (0,)), ((), ())), preferred_element_type=jnp.float32) / math.sqrt(PATS * LEN)
    shape = (PATS, LEN, D)
    return (mixed.reshape(shape), query_grad.reshape(shape), key_grad.reshape(shape), value_grad.reshape(shape), weight_grad)
```

```python
import math

import jax
import jax.numpy as jnp
from jax import lax
from jax.experimental import pallas as pl
from jax.experimental.pallas import tpu as pltpu
from jax.sharding import PartitionSpec as P

HD = 128
MESH = pl.DeviceIdType.MESH
F32 = jnp.float32
BF = jnp.bfloat16


def dot(a, b, ca, cb):
    return lax.dot_general(a, b, (((ca,), (cb,)), ((), ())), preferred_element_type=F32)


def make_kernel(n, np_, rows, width, nb, grad_scale):
    heads = width // HD
    per = heads // np_
    blk = per * HD
    piece = width // n
    m = n // 2
    half_rows = blk // 2
    zrows = half_rows // m
    wrows = blk // 8
    n_go = m if piece % HD == 0 else 1
    n_scan_y = 4 * np_

    def kernel(
        q, k, v, go, w, vm, ln,
        mixed, dq, dk, dv, wg,
        w_all, go_all, att, attc, att_t, sc, allowed, g, dk0, dv0,
        st, sb, rv, sa, box1, pair1, zbox1, px1, pz1, pd1,
        box2, pair2, zbox2, px2, pz2, pd2, part, pbox, psum, zpart,
        lsem, ps, pr, ys, yr, zs, zr,
    ):
        me = lax.axis_index("pat")
        si = lax.axis_index("seq")
        sib = me + 1 - 2 * (me % 2)
        xp = (me + 2) % np_
        diag = (sib + 2) % np_
        yi = si % 2
        zi = si // 2
        yo = 1 - yi
        partner = si + 1 - 2 * yi

        def zpeer(d):
            return ((zi + d) % m) * 2 + yi

        barrier = pltpu.get_barrier_semaphore()
        for peer in (sib, xp, diag):
            pl.semaphore_signal(barrier, inc=1, device_id={"pat": peer}, device_id_type=MESH)
        for peer in [partner] + [zpeer(d) for d in range(1, m)]:
            pl.semaphore_signal(barrier, inc=1, device_id={"seq": peer}, device_id_type=MESH)
        pl.semaphore_wait(barrier, 3 + m)

        def pat_copy(src, dst, i, peer):
            return pltpu.make_async_remote_copy(
                src_ref=src, dst_ref=dst, send_sem=ps.at[i], recv_sem=pr.at[i],
                device_id={"pat": peer}, device_id_type=MESH,
            )

        def y_copy(src, dst, i):
            return pltpu.make_async_remote_copy(
                src_ref=src, dst_ref=dst, send_sem=ys.at[i], recv_sem=yr.at[i],
                device_id={"seq": partner}, device_id_type=MESH,
            )

        def z_copy(src, dst, i, d):
            return pltpu.make_async_remote_copy(
                src_ref=src, dst_ref=dst, send_sem=zs.at[i, d], recv_sem=zr.at[i, d],
                device_id={"seq": zpeer(d)}, device_id_type=MESH,
            )

        local_w = pltpu.make_async_copy(w, w_all.at[me], lsem.at[0])
        local_go = pltpu.make_async_copy(go, go_all.at[me], lsem.at[1])
        w_sib = pat_copy(w, w_all.at[me], 0, sib)
        go_sib = pat_copy(go, go_all.at[me], 1, sib)
        att_out = [
            pat_copy(att.at[peer], attc.at[me], 2 + i, peer) for i, peer in enumerate((xp, diag, sib))
        ]

        def go_cols(d):
            if n_go == 1:
                return slice(None)
            return pl.ds(pl.multiple_of(((zi + d + 1) % m) * 2 * piece, HD), 2 * piece)

        go_x = [
            pat_copy(go.at[:, go_cols(d)], go_all.at[me, :, go_cols(d)], 5 + d, xp)
            for d in range(n_go)
        ]
        go_relay = [
            pat_copy(go_all.at[xp, :, go_cols(d)], go_all.at[xp, :, go_cols(d)], 5 + n_go + d, sib)
            for d in range(n_go)
        ]
        zb = zi % 2
        zpair = (zi + 1 - 2 * zb) * 2 + yi
        base_w = 5 + 2 * n_go

        def unit(y, z, h):
            at = ((y * 2 + z) * 2 + h) * wrows
            return pl.ds(pl.multiple_of(at, wrows), wrows)

        def zpair_copy(src, i):
            return pltpu.make_async_remote_copy(
                src_ref=src, dst_ref=src, send_sem=lsem.at[2 + i], recv_sem=lsem.at[5 + i],
                device_id={"seq": zpair}, device_id_type=MESH,
            )

        spots = [
            unit(yi, zb, 0), unit(yi, zb, 1), unit(yi, 1 - zb, 0), unit(yi, 1 - zb, 1),
            unit(yo, zb, 0), unit(yo, zb, 1), unit(yo, 1 - zb, 0), unit(yo, 1 - zb, 1),
        ]
        near = [w_all.at[xp, spot] for spot in spots]
        w_x = [pat_copy(w.at[spots[i]], w_all.at[me, spots[i]], base_w + i, xp) for i in range(2)]
        w_relay = [pat_copy(near[c], near[c], base_w + 2 + c, sib) for c in range(8)]
        w_z = [zpair_copy(near[c], i) for i, c in enumerate((0, 1, 5))]
        w_y = [y_copy(near[c], near[c], n_scan_y + i) for i, c in enumerate((0, 1, 2))]

        w_x[0].start()
        w_x[1].start()
        go_x[0].start()
        w_sib.start()
        go_sib.start()
        local_w.start()
        local_go.start()

        pos_c = si * rows + lax.broadcasted_iota(jnp.int32, (rows, 1), 0)
        pos_r = si * rows + lax.broadcasted_iota(jnp.int32, (1, rows), 1)
        live = jnp.where(pos_c < ln[0], 1.0, 0.0).astype(F32)
        live_r = jnp.where(pos_r < ln[0], 1.0, 0.0).astype(F32)
        live_h = live.astype(BF)
        scale = live * lax.rsqrt((pos_c + 1).astype(F32)) / math.sqrt(HD)

        def lanes(pb, i, size=HD):
            return pl.ds(pl.multiple_of(pb * blk + i * HD, HD), size)

        def half(pb, y):
            return pl.ds(pl.multiple_of(pb * blk + y * half_rows, half_rows), half_rows)

        def z_of(i):
            return pl.ds(pl.multiple_of(i * zrows, zrows), zrows)

        def wait(copies):
            for copy in copies:
                copy.wait()

        class Scan:
            def __init__(self, own, dst, bufs, g, pb, base, forward):
                self.own, self.dst, self.pb = own, dst, pb
                self.box, self.pair, self.zbox, self.px, self.pz, self.pd = [b.at[g] for b in bufs]
                self.forward = forward
                self.order = range(m) if forward else range(m - 1, -1, -1)
                self.a = y_copy(own.at[half(pb, yo)], self.box, base)
                self.b = [
                    z_copy(self.pair.at[z_of((zi + d) % m)], self.zbox.at[zi], base, d)
                    for d in range(1, m)
                ]
                self.c = [
                    z_copy(self.px.at[(zi + d) % m], self.pz.at[z_of(zi)], base + 1, d)
                    for d in range(1, m)
                ]
                self.d = y_copy(self.pd, dst.at[half(pb, yi)], base + 1)

            def run_a(self):
                self.a.start()

            def run_b(self):
                self.a.wait()
                both = self.own[half(self.pb, yi), :].astype(F32) + self.box[...].astype(F32)
                self.pair[...] = both.astype(BF)
                for copy in self.b:
                    copy.start()
                self.zbox[zi] = self.pair[z_of(zi), :]

            def run_c(self):
                wait(self.b)
                total = jnp.zeros((zrows, HD), F32)
                for s in self.order:
                    self.px[s] = total.astype(BF)
                    total = total + self.zbox[s].astype(F32)
                for copy in self.c:
                    copy.start()
                self.pz[z_of(zi), :] = self.px[zi]

            def run_d(self):
                wait(self.c)
                late = (yi if self.forward else yo).astype(F32)
                mine = half(self.pb, yi)
                base = self.pz[...].astype(F32)
                give = base + (1.0 - late) * self.own[mine, :].astype(F32)
                self.pd[...] = give.astype(BF)
                self.d.start()
                keep = base + late * self.box[...].astype(F32)
                self.dst[mine, :] = keep.astype(BF)

        order_f = (xp, diag, sib, me)
        order_b = (me, sib, xp, diag)
        bufs_f = (box1, pair1, zbox1, px1, pz1, pd1)
        bufs_b = (box2, pair2, zbox2, px2, pz2, pd2)
        fwd = [Scan(st, sb, bufs_f, g, pb, 2 * g, True) for g, pb in enumerate(order_f)]
        bwd = [Scan(rv, sa, bufs_b, g, pb, 2 * (np_ + g), False) for g, pb in enumerate(order_b)]

        for step, pb in enumerate(order_f):
            for i in range(per):
                ls = lanes(pb, i)
                st[ls, :] = dot(k[:, ls] * live_h, v[:, ls], 0, 0).astype(BF)
            fwd[step].run_a()

        row_i = lax.broadcasted_iota(jnp.int32, (rows, rows), 0)
        col_i = lax.broadcasted_iota(jnp.int32, (rows, rows), 1)
        rb, cb = row_i // (rows // nb), col_i // (rows // nb)
        keep = jnp.where(rb == cb, 1.0, 0.0).astype(F32)
        for i in range(nb):
            for j in range(i):
                on = jnp.where(vm[0, 0, i, j] == 1, 1.0, 0.0).astype(F32)
                keep = keep + jnp.where((rb == i) & (cb == j), on, 0.0)
        allowed[...] = jnp.where(row_i >= col_i, keep, 0.0) * live * live_r

        def scores(pb):
            for i in range(per):
                ls = lanes(pb, i)
                s = dot(q[:, ls], k[:, ls], 1, 1) * allowed[...]
                sc[pb * per + i] = s.astype(BF)

        def grad_block(pb):
            @pl.loop(0, blk // 256)
            def _(c):
                at = pl.ds(pl.multiple_of(c * 256, 256), 256)
                ga = dot(go[...], w_all[pb, at, :], 1, 1).astype(BF)
                gg = (scale * ga.astype(F32)).astype(BF)
                g[:, pl.ds(pl.multiple_of(pb * blk + c * 256, HD), 256)] = gg
                for i in range(256 // HD):
                    ls = pl.ds(pl.multiple_of(pb * blk + c * 256 + i * HD, HD), HD)
                    rv[ls, :] = dot(q[:, ls], gg[:, i * HD : (i + 1) * HD], 0, 0).astype(BF)

        def attend(pb):
            for i in range(per):
                ls = lanes(pb, i)
                inner = dot(sc[pb * per + i], v[:, ls], 1, 0) + dot(q[:, ls], sb[ls, :], 1, 0)
                att[pb, :, i * HD : (i + 1) * HD] = (scale * inner).astype(BF)

        def grads(pb):
            for i in range(per):
                ls = lanes(pb, i)
                gh = g[:, ls]
                inner = (dot(gh, v[:, ls], 1, 1) * allowed[...]).astype(BF)
                dq[:, ls] = (dot(inner, k[:, ls], 1, 0) + dot(gh, sb[ls, :], 1, 1)).astype(BF)
                dk0[:, ls] = dot(inner, q[:, ls], 0, 0)
                dv0[:, ls] = dot(sc[pb * per + i], gh, 0, 0)

        def finish(pb):
            for i in range(per):
                ls = lanes(pb, i)
                dk[:, ls] = (dk0[:, ls] + live * dot(v[:, ls], sa[ls, :], 1, 1)).astype(BF)
                dv[:, ls] = (dv0[:, ls] + live * dot(k[:, ls], sa[ls, :], 1, 0)).astype(BF)

        def product(cols):
            acc = dot(att_t[0], go_all[0, :, cols], 1, 0)
            for b in range(1, np_):
                acc = acc + dot(att_t[b], go_all[b, :, cols], 1, 0)
            return acc

        def cols_of(i):
            return pl.ds(pl.multiple_of(i * piece, HD), piece)

        def to_of(d):
            return (zi + d + 1) % m

        y_out = [y_copy(part.at[to_of(d) * 2 + yo], pbox.at[to_of(d)], n_scan_y + 3 + d) for d in range(m)]
        z_out = [z_copy(psum.at[to_of(d)], zpart.at[zi], 4 * np_, d + 1) for d in range(m - 1)]

        def y_part(d):
            to = to_of(d)
            if n_go > 1:
                part[to * 2 + yo] = product(cols_of(to * 2 + yo)).astype(BF)
            y_out[d].start()

        def z_part(d):
            to = to_of(d)
            if n_go > 1:
                acc = product(cols_of(to * 2 + yi))
            else:
                acc = part[to * 2 + yi].astype(F32)
            y_out[d].wait()
            acc = acc + pbox[to].astype(F32)
            psum[to] = acc.astype(BF)
            if d < m - 1:
                z_out[d].start()
            else:
                zpart[zi] = psum[to]

        def got_go(d):
            go_x[d].wait()
            go_relay[d].start()

        for i, pb in enumerate(order_f):
            scores(pb)
            fwd[i].run_b()
        local_w.wait()
        w_x[0].wait()
        w_z[0].start()
        w_y[0].start()
        w_relay[0].start()
        grad_block(me)
        bwd[0].run_a()
        fwd[0].run_c()
        fwd[1].run_c()
        w_sib.wait()
        grad_block(sib)
        bwd[1].run_a()
        fwd[2].run_c()
        fwd[3].run_c()
        w_x[1].wait()
        w_y[1].start()
        w_z[1].start()
        w_relay[1].start()
        for i in range(np_):
            fwd[i].run_d()
        bwd[0].run_b()
        bwd[1].run_b()
        w_z[0].wait()
        w_y[2].start()
        w_relay[2].start()
        if n_go > 1:
            go_x[1].start()
        for i, pb in enumerate(order_f):
            fwd[i].d.wait()
            attend(pb)
            if i < 3:
                att_out[i].start()
            if i == 1:
                for d in range(2, n_go):
                    go_x[d].start()
        bwd[0].run_c()
        bwd[1].run_c()
        w_y[1].wait()
        w_z[2].start()
        w_relay[5].start()
        w_y[0].wait()
        w_relay[4].start()
        grads(me)
        w_z[1].wait()
        w_relay[3].start()
        bwd[0].run_d()
        bwd[1].run_d()
        got_go(0)
        att_t[me] = att[me].T
        local_go.wait()
        go_sib.wait()
        w_y[2].wait()
        w_relay[6].start()
        grads(sib)
        w_z[2].wait()
        w_relay[7].start()
        grad_block(xp)
        bwd[2].run_a()
        wait(w_relay)
        grad_block(diag)
        bwd[3].run_a()
        for copy, peer in zip(att_out, (xp, diag, sib)):
            copy.wait()
            att_t[peer] = attc[peer].T
        go_relay[0].wait()
        if n_go == 1:
            for j in range(width // 256):
                acc = product(slice(j * 256, (j + 1) * 256))
                for i in range(256 // piece):
                    part[j * (256 // piece) + i] = acc[:, i * piece : (i + 1) * piece].astype(BF)
            for d in range(m):
                y_part(d)
            bwd[2].run_b()
            bwd[3].run_b()
            grads(xp)
            bwd[2].run_c()
            bwd[3].run_c()
            grads(diag)
            for d in range(m):
                z_part(d)
        else:
            y_part(0)
            bwd[2].run_b()
            grads(xp)
            bwd[3].run_b()
            got_go(1)
            go_relay[1].wait()
            y_part(1)
            bwd[2].run_c()
            z_part(0)
            grads(diag)
            bwd[3].run_c()
            for d in range(2, m):
                got_go(d)
                go_relay[d].wait()
                y_part(d)
                z_part(d - 1)
        bwd[2].run_d()
        bwd[3].run_d()
        if n_go > 1:
            z_part(m - 1)

        @pl.loop(0, width // 256)
        def _(j):
            cols = pl.ds(pl.multiple_of(j * 256, 256), 256)
            acc = dot(att[0], w_all[0, :, cols], 1, 0)
            for b in range(1, np_):
                acc = acc + dot(att[b], w_all[b, :, cols], 1, 0)
            mixed[:, cols] = acc.astype(BF)

        for i, pb in enumerate(order_b):
            bwd[i].d.wait()
            finish(pb)
        wait(z_out)
        total = zpart[0].astype(F32)
        for s in range(1, m):
            total = total + zpart[s].astype(F32)
        wg[...] = total * grad_scale

    vmem = pltpu.VMEM
    sems = pltpu.SemaphoreType.DMA
    state = vmem((heads * HD, HD), BF)
    half_state = vmem((np_, half_rows, HD), BF)
    by_z = vmem((np_, m, zrows, HD), BF)
    scan_boxes = [half_state, half_state, by_z, by_z, half_state, half_state]
    n_pat = 15 + 2 * n_go
    n_y = n_scan_y + 3 + m
    scratch = [
        vmem((np_, blk, width), BF),
        vmem((np_, rows, width), BF),
        vmem((np_, rows, blk), BF),
        vmem((np_, rows, blk), BF),
        vmem((np_, blk, rows), BF),
        vmem((heads, rows, rows), BF),
        vmem((rows, rows), F32),
        vmem((rows, width), BF),
        vmem((rows, width), F32),
        vmem((rows, width), F32),
        state, state, state, state,
        *scan_boxes,
        *scan_boxes,
        vmem((n, blk, piece), BF),
        vmem((m, blk, piece), BF),
        vmem((m, blk, piece), BF),
        vmem((m, blk, piece), BF),
        sems((8,)),
        sems((n_pat,)), sems((n_pat,)),
        sems((n_y,)), sems((n_y,)),
        sems((4 * np_ + 1, m)), sems((4 * np_ + 1, m)),
    ]
    full = jax.ShapeDtypeStruct((rows, width), BF)
    whole = pl.BlockSpec(memory_space=pltpu.VMEM)
    scalar = pl.BlockSpec(memory_space=pltpu.SMEM)
    return pl.pallas_call(
        kernel,
        out_shape=(full, full, full, full, jax.ShapeDtypeStruct((blk, piece), F32)),
        in_specs=[whole] * 5 + [scalar] * 2,
        out_specs=(whole,) * 5,
        scratch_shapes=scratch,
        compiler_params=pltpu.CompilerParams(
            collective_id=0, has_side_effects=True, vmem_limit_bytes=60 * 1024 * 1024
        ),
    )


def solution(mesh):
    n, np_ = mesh.shape["seq"], mesh.shape["pat"]

    def on_device(queries, key_rows, value_rows, out_weight, grad_out, visit_mask, lengths):
        rows, width = queries.shape[1:]
        call = make_kernel(
            n, np_, rows, width, visit_mask.shape[-1], 1.0 / math.sqrt(np_ * n * rows)
        )
        mixed, dq, dk, dv, wg = call(
            queries[0], key_rows[0], value_rows[0], grad_out[0], out_weight, visit_mask, lengths
        )
        return mixed[None], dq[None], dk[None], dv[None], wg

    rows3 = P("pat", "seq", None)
    return jax.shard_map(
        on_device,
        mesh=mesh,
        in_specs=(rows3, rows3, rows3, P("pat", None), rows3, P("pat", "seq", None, None), P("pat")),
        out_specs=(rows3, rows3, rows3, rows3, P("pat", "seq")),
        check_vma=False,
    )
```
